128 devices in a mesh: leaf: 8 (over y_lo, z), front: 16 (over y_hi, x, core).
Axes of the slice: x: 4, y: 4 (y_hi: 2, y_lo: 2; y = y_hi * 2 + y_lo), z: 4, core: 2. Of those that a mesh axis runs over, the one named last changes fastest.
Arguments:
- child_update: float32 [8, 4096, 4096], P('leaf', 'front'), may hold values from -6 to 6
- assembly: int32 [8, 32], replicated, may hold values from 0 to 127, as said below
- front_matrix: float32 [16384, 16384], P('leaf', 'front'), may hold values from -6 to 6
- block_inv: float32 [2, 128, 128], replicated, as said below
Outputs:
- factored: float32 [16384, 16384], P('leaf', 'front')
The draws below stay inside these ranges and needn't reach their ends.
Inputs may be any that keep to these rules, and one draw needn't show every extreme that they name: `assembly`: each row lists 32 distinct parent block indices in increasing order. Of one row's entries, at most 4 lie among the parent blocks whose columns one index of the front axis holds; in every row, all such groups that make up the rows of one index of the leaf axis hold exactly 4 each. `block_inv`: each block is lower triangular with a nonzero diagonal.
All inputs are finite; a program needn't handle non-finite values.
Results may differ from the reference program's by a relative error of at most 0.0001.
Values sent between devices are 32-bit elements; how exact they have to be, the bound alone decides.
No kernel may reach another device: no remote copies, remote signals or barrier semaphores. Data moves between devices by JAX's collectives and lax.ppermute only.
A program may use at most 192 MiB of HBM per device.

```python
import math
import jax
import jax.numpy as jnp
from jax import lax

BLK = 128
FT = 16384
UM = 4096
NPAN = 2
CAPF = 4
GROUPS = 8
UB = 32
N_LEAF = 8
N_FRONT = 16


def assembly_row(key):
    key_offsets, key_leaf, key_order = jax.random.split(key, 3)
    col_blocks = FT // BLK // N_FRONT
    per_leaf = N_FRONT // N_LEAF
    scores = jax.random.randint(key_offsets, (N_FRONT, col_blocks), 0, 1 << 20) * col_blocks + jnp.arange(col_blocks, dtype=jnp.int32)[None, :]
    chosen_offsets = lax.top_k(scores, CAPF)[1].astype(jnp.int32)
    candidates = (jnp.arange(N_FRONT, dtype=jnp.int32)[:, None] * col_blocks + chosen_offsets).reshape(-1)
    full_leaf = jax.random.randint(key_leaf, (), 0, N_LEAF)
    owners = jnp.repeat(jnp.arange(N_FRONT, dtype=jnp.int32), CAPF) // per_leaf
    slot_total = N_FRONT * CAPF
    priority = jax.random.randint(key_order, (slot_total,), 0, 1 << 20) * slot_total + jnp.arange(slot_total, dtype=jnp.int32)
    priority = jnp.where(owners == full_leaf, (1 << 30) + jnp.arange(slot_total, dtype=jnp.int32), priority)
    picked = lax.top_k(priority, UB)[1]
    return jnp.sort(candidates[picked]).astype(jnp.int32)


def draw_assembly(key, part):
    group_keys = jax.random.split(key, GROUPS)
    return jax.vmap(assembly_row)(group_keys).astype(jnp.int32)


def draw_block_inv(key, part):
    key_diag, key_low = jax.random.split(key)
    diagonal = jax.random.uniform(key_diag, (NPAN, BLK), minval=0.5, maxval=1.5)
    lower = jax.random.normal(key_low, (NPAN, BLK, BLK)) / math.sqrt(BLK)
    row_ids = lax.broadcasted_iota(jnp.int32, (BLK, BLK), 0)
    col_ids = lax.broadcasted_iota(jnp.int32, (BLK, BLK), 1)
    strict = jnp.where((row_ids > col_ids)[None], lower, 0.0)
    on_diagonal = jnp.where((row_ids == col_ids)[None], diagonal[:, :, None], 0.0)
    return ((strict + on_diagonal) * 0.125).astype(jnp.float32)


def level_of(own_key, dims, cuts, low, largest):
    def one(dim, blocks):
        steps = jax.random.uniform(jax.random.fold_in(jax.random.fold_in(own_key, 6), dim), (blocks,), jnp.float32, low / len(cuts), largest / len(cuts))
        return jnp.repeat(jnp.exp(steps), dims[dim] // blocks).reshape((-1,) + (1,) * (len(dims) - dim - 1))

    factor_of = one(*cuts[0])
    for cut in cuts[1:]:
        factor_of = factor_of * one(*cut)
    return factor_of


def normal_values(own_key, dims, spread, bound, cuts=(), kind=jnp.bfloat16):
    array = spread * jax.random.normal(own_key, dims, jnp.float32)
    if cuts:
        array = array * level_of(own_key, dims, cuts, -0.22, 0.18)
    return jnp.clip(array, -bound, bound).astype(kind)


def setup_inputs(seed: int = 0) -> dict:
    key_list = jax.random.split(jax.random.key(seed), 5)
    return {
        "child_update": normal_values(key_list[0], (GROUPS, UM, UM), 1.0, 6.0, ((0, 8), (1, 16)), jnp.float32),
        "assembly": draw_assembly(jax.random.fold_in(key_list[4], 71), 0),
        "front_matrix": normal_values(key_list[2], (FT, FT), 1.0, 6.0, ((0, 8), (1, 16)), jnp.float32),
        "block_inv": draw_block_inv(jax.random.fold_in(key_list[4], 71), 0),
    }


def reference(child_update, assembly, front_matrix, block_inv):
    highest = lax.Precision.HIGHEST
    offsets = jnp.arange(BLK, dtype=jnp.int32)
    assembled = front_matrix
    for member in range(GROUPS):
        positions = (assembly[member][:, None] * BLK + offsets[None, :]).reshape(-1).astype(jnp.int32)
        assembled = assembled.at[positions[:, None], positions[None, :]].add(child_update[member])
    row_ids = jnp.arange(FT, dtype=jnp.int32)
    pieces = []
    for panel_step in range(NPAN):
        columns = assembled[:, panel_step * BLK:(panel_step + 1) * BLK]
        factor = jnp.dot(columns, jnp.transpose(block_inv[panel_step]), precision=highest)
        factor = jnp.where((row_ids >= panel_step * BLK)[:, None], factor, jnp.zeros_like(factor))
        assembled = assembled - jnp.dot(factor, jnp.transpose(factor), precision=highest)
        pieces.append(factor)
    return jnp.concatenate(pieces + [assembled[:, NPAN * BLK:]], axis=1)
```

```python
import functools

import jax
import jax.numpy as jnp
from jax import lax
from jax.experimental import pallas as pl
from jax.experimental.pallas import tpu as pltpu
from jax.sharding import PartitionSpec as P

BLK = 128
CAPF = 4
UB = 32
CHUNKS = tuple((c, 0, 128) for c in range(CAPF))

T_R, T_RANK, T_M, T_ROWU, T_PROW, T_VCOL, T_ALL = 128, 384, 640, 768, 832, 960, 1024

HBM = pl.BlockSpec(memory_space=pltpu.HBM)
SMEM = pl.BlockSpec(memory_space=pltpu.SMEM)
COST = pl.CostEstimate(flops=1000, bytes_accessed=1 << 20, transcendentals=0)


def leaf_at(y_lo, z):
    return y_lo % 2 * 4 + z % 4


def front_at(y_hi, x, core):
    return y_hi % 2 * 8 + x % 4 * 2 + core % 2


def device_at(leaf, front):
    return leaf * 16 + front


def copy(src, dst, sem):
    return pltpu.make_async_copy(src, dst, sem)


def call(body, operands, outs, name):
    n = len(outs)

    def kernel(*refs):
        ins, results, held, sem = refs[:-n - 2], refs[-n - 2:-2], refs[-2], refs[-1]
        body(ins, held, sem)
        writes = [copy(held.at[k], results[k], sem) for k in range(n)]
        for w in writes:
            w.start()
        for w in writes:
            w.wait()

    return pl.pallas_call(
        kernel,
        out_shape=[jax.ShapeDtypeStruct(s, jnp.float32) for s in outs],
        in_specs=[SMEM] + [HBM] * (len(operands) - 1),
        out_specs=[HBM] * n,
        scratch_shapes=[pltpu.VMEM((n,) + outs[0], jnp.float32), pltpu.SemaphoreType.DMA(())],
        compiler_params=pltpu.CompilerParams(vmem_limit_bytes=12 << 20),
        cost_estimate=COST,
        name=name,
    )(*operands)


def own_columns(meta, act):
    def column(j, carry):
        before, rank = carry
        owner = meta[j] >> 3
        rank = jnp.where(owner == before, rank + 1, 0)
        act(j, owner, rank)
        return owner, rank

    lax.fori_loop(0, UB, column, (jnp.int32(-1), jnp.int32(0)))


def pack_core(c, meta, child, after):
    def body(ins, held, sem):
        meta, child = ins[:2]
        core = meta[UB + 1] & 1
        for wait in (False, True):
            def act(j, owner, rank, wait=wait):
                @pl.when((rank == c) & ((owner & 1) != core))
                def _():
                    columns = pl.ds(pl.multiple_of(j * BLK, BLK), BLK)
                    one = copy(child.at[:, :, columns], held.at[0, owner >> 1], sem)
                    one.wait() if wait else one.start()

            own_columns(meta, act)

    return call(body, [meta, child] + after, [(8, 2, BLK, BLK)], "pack_core")


def pack_x(chunk, meta, child, crossed, after):
    c, off, rows = chunk

    def body(ins, held, sem):
        meta, child, crossed = ins[:3]
        front = meta[UB + 1]
        x, core = (front >> 1) & 3, front & 1
        part = pl.ds(off, rows)
        for wait in (False, True):
            def act(j, owner, rank, wait=wait):
                @pl.when((rank == c) & ((owner & 1) == core))
                def _():
                    target = ((owner >> 1) - x) & 3
                    columns = pl.ds(pl.multiple_of(j * BLK, BLK), BLK)
                    one = copy(child.at[:, part, columns], held.at[target, owner >> 3, 0], sem)
                    two = copy(crossed.at[owner >> 1, :, part], held.at[target, owner >> 3, 1], sem)
                    for d in (one, two):
                        d.wait() if wait else d.start()

            own_columns(meta, act)

    return call(body, [meta, child, crossed] + after, [(2, 2, 2, rows, BLK)] * 4, "pack_x")


def pack_y(chunk, tab, arrays, after):
    c, _, rows = chunk

    def body(ins, held, sem):
        tab, arrays = ins[0], ins[1:5]
        leaf, front = tab[0], tab[1]
        y_hi, x, core = front >> 3, (front >> 1) & 3, front & 1
        y = y_hi * 2 + (leaf >> 2)
        for wait in (False, True):
            for to_hi in range(2):
                @pl.when(tab[T_M + leaf * 16 + to_hi * 8 + (front & 7)] > c)
                def _():
                    for k in range(4):
                        def one(n, carry):
                            other, r = n >> 1, n & 1
                            slot = (((x - k) & 3) * 2 + (core ^ other)) * 2 + r
                            owner = tab[T_R + leaf * UB + y_hi * 16 + slot]
                            target = (to_hi * 2 + (owner >> 2) - y) & 3
                            d = copy(arrays[k].at[to_hi, other, r], held.at[target, slot], sem)
                            d.wait() if wait else d.start()
                            return carry

                        lax.fori_loop(0, 4, one, 0)

    return call(body, [tab] + arrays + after, [(16, rows, BLK)] * 4, "pack_y")


def pack_z(chunk, tab, arrays, after):
    c, _, rows = chunk

    def body(ins, held, sem):
        tab, arrays = ins[0], ins[1:5]
        leaf, front = tab[0], tab[1]
        z, y_lo = leaf & 3, leaf >> 2
        y = (front >> 3) * 2 + y_lo
        for wait in (False, True):
            for k in range(4):
                source = (y - k) & 3
                from_lo = source & 1
                group = from_lo * 4 + z

                @pl.when(tab[T_M + group * 16 + front] > c)
                def _():
                    def one(s, carry):
                        i = group * UB + (source >> 1) * 16 + s
                        owner = tab[T_R + i]

                        @pl.when((owner >> 2) == y_lo)
                        def _():
                            d = copy(arrays[k].at[s], held.at[(owner - z) & 3, from_lo, tab[T_RANK + i]], sem)
                            d.wait() if wait else d.start()

                        return carry

                    lax.fori_loop(0, 16, one, 0)

    return call(body, [tab] + arrays + after, [(2, 8, rows, BLK)] * 4, "pack_z")


def panel_sum(chunks, tab, front_tile, arrays):
    n_arrays = 4 * len(chunks)

    def kernel(tab, tile, *refs):
        arrays, outs, (total, held, sem) = refs[:n_arrays], refs[n_arrays:-3], refs[-3:]
        z = tab[0] & 3

        def each(act):
            for n, (c, off, rows) in enumerate(chunks):
                for k in range(4):
                    for lo in range(2):
                        group = lo * 4 + ((z - k) & 3)
                        v = tab[T_VCOL + group * 4 + c]

                        @pl.when((v >= 0) & (v < 2))
                        def _():
                            def one(p, carry):
                                u = tab[T_ROWU + group * 8 + p]

                                @pl.when(u >= 0)
                                def _():
                                    act(arrays[n * 4 + k].at[lo, p], held.at[c, k * 2 + lo, p, pl.ds(off, rows)], u, v, off, rows)

                                return carry

                            lax.fori_loop(0, 8, one, 0)

        @pl.when(tab[1] == 0)
        def _():
            whole = copy(tile.at[:, pl.ds(0, 2 * BLK)], total, sem)
            whole.start()
            each(lambda src, dst, *_: copy(src, dst, sem).start())
            whole.wait()
            each(lambda src, dst, *_: copy(src, dst, sem).wait())

            def add(src, dst, u, v, off, rows):
                at = (pl.ds(pl.multiple_of(u * BLK + off, 64), rows), pl.ds(pl.multiple_of(v * BLK, BLK), BLK))
                total[at] += dst[...]

            each(add)
            out = [copy(total.at[pl.ds(q * 512, 512)], outs[q], sem) for q in range(4)]
            out.append(copy(total.at[pl.ds(BLK, BLK), pl.ds(0, BLK)], outs[4], sem))
            for o in out:
                o.start()
            for o in out:
                o.wait()

    return pl.pallas_call(
        kernel,
        out_shape=[jax.ShapeDtypeStruct((512, 2 * BLK), jnp.float32)] * 4 + [jax.ShapeDtypeStruct((BLK, BLK), jnp.float32)],
        in_specs=[SMEM] + [HBM] * (n_arrays + 1),
        out_specs=[HBM] * 5,
        scratch_shapes=[
            pltpu.VMEM((2048, 2 * BLK), jnp.float32),
            pltpu.VMEM((2, 8, 8, BLK, BLK), jnp.float32),
            pltpu.SemaphoreType.DMA(()),
        ],
        compiler_params=pltpu.CompilerParams(vmem_limit_bytes=24 << 20),
        cost_estimate=COST,
        name="panel_sum",
    )(tab, front_tile, *arrays)


def column_rows(tab, quarters):
    def body(ins, held, sem):
        tab, quarters = ins[0], ins[1:5]
        front = tab[1]
        x, core = (front >> 1) & 3, front & 1
        for wait in (False, True):
            for n in range(4):
                at = (x - core * 2 - n // 2) & 3
                for k in range(4):
                    @pl.when(at == k)
                    def _():
                        d = copy(quarters[k].at[pl.ds(n % 2 * 256, 256)], held.at[n], sem)
                        d.wait() if wait else d.start()

    return call(body, [tab] + quarters, [(256, 2 * BLK)] * 4, "column_rows")


def product(a, b, precision=lax.Precision.HIGHEST):
    return lax.dot_general(a, b, (((1,), (1,)), ((), ())), precision=precision, preferred_element_type=jnp.float32)


def final(tab, front_tile, block_inv, corner, arrays, quarters, pieces):
    n_arrays = 4 * len(CHUNKS)
    steps = front_tile.shape[0] // BLK
    width = front_tile.shape[1]

    def kernel(tab, tile, inv, corner, *refs):
        arrays, quarters, pieces = refs[:n_arrays], refs[n_arrays:n_arrays + 4], refs[n_arrays + 4:n_arrays + 8]
        out, held, rows_in, columns_in, right, sems, column_sem = refs[n_arrays + 8:]
        u = pl.program_id(0)
        leaf, front = tab[0], tab[1]
        z, x = leaf & 3, (front >> 1) & 3

        def each(step, act):
            for k in range(4):
                for lo in range(2):
                    group = lo * 4 + ((z - k) & 3)
                    p = tab[T_PROW + group * 16 + step]

                    @pl.when(p >= 0)
                    def _():
                        for c in range(CAPF):
                            v = tab[T_VCOL + group * 4 + c]

                            @pl.when(v >= 0)
                            def _():
                                act(k, lo, p, c, v)

        def fetch(step, wait):
            slot = step & 1
            sem = sems.at[slot]

            def act(k, lo, p, c, v):
                for n, (cc, off, rows) in enumerate(CHUNKS):
                    if cc == c:
                        one = copy(arrays[n * 4 + k].at[lo, p], held.at[slot, k * 2 + lo, c, pl.ds(off, rows)], sem)
                        one.wait() if wait else one.start()

            each(step, act)
            at = (x - (step >> 2)) & 3
            for k in range(4):
                @pl.when(at == k)
                def _():
                    one = copy(
                        quarters[k].at[pl.ds(pl.multiple_of((step & 3) * BLK, BLK), BLK)], rows_in.at[slot], sem
                    )
                    one.wait() if wait else one.start()

        def panels(raw, first):
            left = product(raw[:, :BLK], inv[0])
            below = product(corner[...], inv[0])
            second = product(raw[:, BLK:] - product(left, below), inv[1])
            return left, jnp.where(first, 0.0, second)

        @pl.when(u == 0)
        def _():
            fetch(0, False)
            for wait in (False, True):
                for k in range(4):
                    n = (z - k - (front >> 1)) & 3
                    one = copy(pieces[k], columns_in.at[pl.ds(pl.multiple_of(n * 256, 256), 256)], column_sem)
                    one.wait() if wait else one.start()
            for n in range(width // BLK):
                rows = pl.ds(n * BLK, BLK)
                left, second = panels(columns_in[rows], (front == 0) & (n == 0))
                for h, part in enumerate((left, second)):
                    high = part.astype(jnp.bfloat16)
                    low = (part - high.astype(jnp.float32)).astype(jnp.bfloat16)
                    for m, value in enumerate((high, high, low)):
                        right[rows, pl.ds((m * 2 + h) * BLK, BLK)] = value

        @pl.when(u + 1 < steps)
        def _():
            fetch(u + 1, False)

        fetch(u, True)
        slot = u & 1
        left, second = panels(rows_in[slot], (leaf == 0) & (u == 0))
        high, low = [], []
        for part in (left, second):
            high.append(part.astype(jnp.bfloat16))
            low.append((part - high[-1].astype(jnp.float32)).astype(jnp.bfloat16))
        split = jnp.concatenate(high + low + high, axis=1)
        out[...] = tile[...] - product(split, right[...], None)

        def add(k, lo, p, c, v):
            columns = pl.ds(pl.multiple_of(v * BLK, BLK), BLK)
            out[:, columns] += held[slot, k * 2 + lo, c]

        each(u, add)

        @pl.when(front == 0)
        def _():
            out[:, pl.ds(0, BLK)] = left
            out[:, pl.ds(BLK, BLK)] = second

    return pl.pallas_call(
        kernel,
        out_shape=jax.ShapeDtypeStruct(front_tile.shape, jnp.float32),
        grid=(steps,),
        in_specs=[
            SMEM,
            pl.BlockSpec((BLK, width), lambda u: (u, 0)),
            pl.BlockSpec((2, BLK, BLK), lambda u: (0, 0, 0)),
            pl.BlockSpec((BLK, BLK), lambda u: (0, 0)),
        ] + [HBM] * (n_arrays + 8),
        out_specs=pl.BlockSpec((BLK, width), lambda u: (u, 0)),
        scratch_shapes=[
            pltpu.VMEM((2, 8, CAPF, BLK, BLK), jnp.float32),
            pltpu.VMEM((2, BLK, 2 * BLK), jnp.float32),
            pltpu.VMEM((width, 2 * BLK), jnp.float32),
            pltpu.VMEM((width, 6 * BLK), jnp.bfloat16),
            pltpu.SemaphoreType.DMA((2,)),
            pltpu.SemaphoreType.DMA(()),
        ],
        compiler_params=pltpu.CompilerParams(vmem_limit_bytes=32 << 20),
        cost_estimate=COST,
        name="final",
    )(tab, front_tile, block_inv, corner, *arrays, *quarters, *pieces)


def shift_x(a, dx, dc):
    pairs = [
        (front_at(h, x, c), front_at(h, x + dx, c + dc)) for h in range(2) for x in range(4) for c in range(2)
    ]
    return lax.ppermute(a, "front", pairs)


def shift_y(a, dy):
    pairs = []
    for y in range(4):
        to = (y + dy) % 4
        for z in range(4):
            for x in range(4):
                for c in range(2):
                    pairs.append((
                        device_at(leaf_at(y, z), front_at(y // 2, x, c)),
                        device_at(leaf_at(to, z), front_at(to // 2, x, c)),
                    ))
    return lax.ppermute(a, ("leaf", "front"), pairs)


def shift_z(a, dz):
    return lax.ppermute(a, "leaf", [(leaf_at(l, z), leaf_at(l, z + dz)) for l in range(2) for z in range(4)])


def spread(a, steps, axis):
    for step in steps:
        a = functools.reduce(jnp.add, [lax.ppermute(a, axis, pairs) for pairs in step], a)
    return a


def tables(assembly, leaf, front):
    col_owner, row_owner = assembly >> 3, assembly >> 4
    earlier = jnp.arange(UB)[:, None] > jnp.arange(UB)[None, :]

    def rank(owner):
        same = (owner[:, :, None] == owner[:, None, :]) & earlier[None]
        return jnp.sum(same.astype(jnp.int32), axis=2)

    def pick(match, value):
        return jnp.sum(jnp.where(match, value + 1, 0), axis=1).astype(jnp.int32) - 1

    row_rank, col_rank = rank(row_owner), rank(col_owner)
    count = jnp.sum((col_owner[:, :, None] == jnp.arange(16)).astype(jnp.int32), axis=1)
    mine = row_owner == leaf
    row_u = pick(
        mine[:, :, None] & (row_rank[:, :, None] == jnp.arange(8)), (assembly & 15)[:, :, None]
    )
    row_p = pick(assembly[:, :, None] == leaf * 16 + jnp.arange(16), row_rank[:, :, None])
    col_v = pick(
        (col_owner == front)[:, :, None] & (col_rank[:, :, None] == jnp.arange(CAPF)), (assembly & 7)[:, :, None]
    )
    head = jnp.concatenate([leaf[None], front[None], jnp.zeros((T_R - 2,), jnp.int32)])
    parts = [head] + [t.reshape(-1) for t in (row_owner, row_rank, count, row_u, row_p, col_v)]
    size = sum(t.shape[0] for t in parts)
    return jnp.concatenate(parts + [jnp.zeros((T_ALL - size,), jnp.int32)])


def per_device(child_update, assembly, front_matrix, block_inv):
    leaf, front = lax.axis_index("leaf"), lax.axis_index("front")
    child = child_update.reshape(2, BLK, child_update.shape[2])
    own = lax.dynamic_index_in_dim(assembly, leaf, 0, keepdims=False)
    meta = jnp.concatenate([own, leaf[None], front[None], jnp.zeros((94,), jnp.int32)])
    tab = tables(assembly, leaf, front)

    n = len(CHUNKS)
    panel_chunks = [s for s in range(n) if CHUNKS[s][0] < 2]
    x_in, y_in, z_in = [None] * n, [None] * n, [None] * n
    after_x, after_y, after_z = [], [], []

    crossed = [None] * CAPF

    def do_x(s):
        c = CHUNKS[s][0]
        if crossed[c] is None:
            mine = pack_core(c, meta, child, after_x)[0]
            crossed[c] = shift_x(mine, 0, 1)
        outs = pack_x(CHUNKS[s], meta, child, crossed[c], after_x)
        x_in[s] = [outs[0]] + [shift_x(outs[k], k, 0) for k in range(1, 4)]
        return outs

    def do_y(s, after):
        outs = pack_y(CHUNKS[s], tab, x_in[s], after)
        y_in[s] = [outs[0]] + [shift_y(outs[k], k) for k in range(1, 4)]
        return outs

    def do_z(s, after):
        outs = pack_z(CHUNKS[s], tab, y_in[s], after)
        z_in[s] = [outs[0]] + [shift_z(outs[k], k) for k in range(1, 4)]
        return outs

    do_x(0)
    last_z = []
    for s in range(n + 1):
        if s < n:
            y_out = do_y(s, list(last_z[:1]))
            after_x = [y_out[0]]
            if s + 1 < n:
                do_x(s + 1)
        if s >= 1:
            last_z = do_z(s - 1, [y_out[0]])

    sums = panel_sum(
        [CHUNKS[s] for s in panel_chunks], tab, front_matrix, [a for s in panel_chunks for a in z_in[s]]
    )
    sums = [jnp.where(front == 0, a, 0.0) for a in sums]
    both = ("leaf", "front")
    root = front_at(0, 0, 0)
    quarter = sums[0]
    for x in range(1, 4):
        quarter = quarter + lax.ppermute(sums[x], "front", [(root, front_at(0, x, 0))])
    quarter = spread(
        quarter,
        [[[(front_at(0, x, 0), front_at(h, x, c)) for x in range(4)] for h, c in ((0, 1), (1, 0), (1, 1))]],
        "front",
    )
    quarters = [quarter] + [shift_x(quarter, dx, 0) for dx in range(1, 4)]
    roots = [(f // 2, f) for f in range(16)]
    pieces = column_rows(tab, quarters)
    at_root = leaf == front >> 1
    piece = jnp.where(at_root, pieces[0], 0.0)
    for dz in range(1, 4):
        pairs = [(device_at(l, f), device_at(leaf_at(l // 4, l + dz), f)) for l, f in roots]
        piece = piece + lax.ppermute(pieces[dz], both, pairs)
    piece = spread(
        piece,
        [[[
            (device_at(leaf_at(l // 4, z), f), device_at(leaf_at(1 - l // 4, z), f)) for l, f in roots for z in range(4)
        ]]],
        both,
    )
    pieces = [piece] + [shift_z(piece, dz) for dz in range(1, 4)]
    corner = jnp.where(leaf == 0, sums[4], 0.0)
    corner = spread(
        corner,
        [
            [[(device_at(0, root), device_at(leaf_at(0, z), root))] for z in range(1, 4)],
            [[(device_at(leaf_at(0, z), root), device_at(leaf_at(1, z), root)) for z in range(4)]],
            [[(device_at(l, root), device_at(l, front_at(0, x, 0))) for l in range(8)] for x in range(1, 4)],
            [[
                (device_at(l, front_at(0, x, 0)), device_at(l, front_at(h, x, c))) for l in range(8) for x in range(4)
            ] for h, c in ((0, 1), (1, 0), (1, 1))],
        ],
        both,
    )
    arrays = [a for s in range(n) for a in z_in[s]]
    return final(tab, front_matrix, block_inv, corner, arrays, quarters, pieces)


def solution(mesh):
    placed = (P("leaf", "front", None), P(), P("leaf", "front"), P())
    return jax.shard_map(
        per_device, mesh=mesh, in_specs=placed, out_specs=P("leaf", "front"), check_vma=False
    )
```

```python
import functools

import jax
import jax.numpy as jnp
from jax import lax
from jax.experimental import pallas as pl
from jax.experimental.pallas import tpu as pltpu
from jax.sharding import PartitionSpec as P

BLK = 128
CAPF = 4
NPAN = 2
UB = 32
WHOLE = [(c, 0, 128) for c in range(CAPF)]
COUNT = 48

T_R, T_RANK, T_M, T_ROWU, T_PROW, T_VCOL, T_ALL = 128, 384, 640, 768, 832, 960, 1024

HBM = pl.BlockSpec(memory_space=pltpu.HBM)
SMEM = pl.BlockSpec(memory_space=pltpu.SMEM)
COST = pl.CostEstimate(flops=1000, bytes_accessed=1 << 16, transcendentals=0)
VMEM = 60 << 20
STEP = 2


def leaf_at(y_lo, z):
    return y_lo % 2 * 4 + z % 4


def front_at(y_hi, x, core):
    return y_hi % 2 * 8 + x % 4 * 2 + core % 2


def device_at(leaf, front):
    return leaf * 16 + front


def copy(src, dst, sem):
    return pltpu.make_async_copy(src, dst, sem)


def call(body, operands, outs, name):
    n = len(outs)

    def kernel(*refs):
        ins, results, held, sem = refs[:-n - 2], refs[-n - 2:-2], refs[-2], refs[-1]
        body(ins, held, sem)
        writes = [copy(held.at[k], results[k], sem) for k in range(n)]
        for w in writes:
            w.start()
        for w in writes:
            w.wait()

    return pl.pallas_call(
        kernel,
        out_shape=[jax.ShapeDtypeStruct(s, jnp.float32) for s in outs],
        in_specs=[SMEM] + [HBM] * (len(operands) - 1),
        out_specs=[HBM] * n,
        scratch_shapes=[pltpu.VMEM((n,) + outs[0], jnp.float32), pltpu.SemaphoreType.DMA(())],
        compiler_params=pltpu.CompilerParams(vmem_limit_bytes=VMEM),
        cost_estimate=COST,
        name=name,
    )(*operands)


def own_columns(meta, act):
    def column(j, carry):
        before, rank = carry
        owner = meta[j] >> 3
        rank = jnp.where(owner == before, rank + 1, 0)
        act(j, owner, rank)
        return owner, rank

    lax.fori_loop(0, UB, column, (jnp.int32(-1), jnp.int32(0)))


def pack_core(first, last, meta, child):
    def body(ins, held, sem):
        meta, child = ins[:2]
        core = meta[UB + 1] & 1
        for wait in (False, True):
            def act(j, owner, rank, wait=wait):
                @pl.when((rank >= first) & (rank < last) & ((owner & 1) != core))
                def _():
                    columns = pl.ds(pl.multiple_of(j * BLK, BLK), BLK)
                    one = copy(child.at[:, :, columns], held.at[0, rank - first, owner >> 1], sem)
                    one.wait() if wait else one.start()

            own_columns(meta, act)

    return call(body, [meta, child], [(last - first, 8, 2, BLK, BLK)], "pack_core")


def pack_x(first, last, meta, child, crossed, base, after):
    def body(ins, held, sem):
        meta, child, crossed = ins[:3]
        front = meta[UB + 1]
        x, core = (front >> 1) & 3, front & 1
        for wait in (False, True):
            def act(j, owner, rank, wait=wait):
                @pl.when((rank >= first) & (rank < last) & ((owner & 1) == core))
                def _():
                    source = child.at[:, :, pl.ds(pl.multiple_of(j * BLK, BLK), BLK)]
                    d = copy(source, held.at[((owner >> 1) - x) & 3, rank - first, owner >> 3, 0], sem)
                    d.wait() if wait else d.start()

            def other(f, carry, wait=wait):
                for rank in range(first, last):
                    @pl.when(meta[COUNT + f * 2 + core] > rank)
                    def _():
                        d = copy(crossed.at[rank - base, f], held.at[(f - x) & 3, rank - first, f >> 2, 1], sem)
                        d.wait() if wait else d.start()

                return carry

            own_columns(meta, act)
            lax.fori_loop(0, 8, other, 0)

    return call(body, [meta, child, crossed] + after, [(last - first, 2, 2, 2, BLK, BLK)] * 4, "pack_x")


def pack_y(c, tab, arrays, base, extra=None):
    def body(ins, held, sem):
        tab, arrays = ins[0], ins[1:]
        leaf, front = tab[0], tab[1]
        y_hi, x, core = front >> 3, (front >> 1) & 3, front & 1
        for wait in (False, True):
            for to_hi in range(2):
                @pl.when(tab[T_M + leaf * 16 + to_hi * 8 + (front & 7)] > c)
                def _():
                    for k in range(4):
                        def one(n, carry):
                            other, r = n >> 1, n & 1
                            slot = (((x - k) & 3) * 2 + (core ^ other)) * 2 + r
                            owner = tab[T_R + leaf * UB + y_hi * 16 + slot]
                            d = copy(arrays[k].at[c - base, to_hi, other, r], held.at[0, to_hi * 2 + (owner >> 2), slot], sem)
                            d.wait() if wait else d.start()
                            return carry

                        lax.fori_loop(0, 4, one, 0)

            if extra is not None:
                to = held.at[0, (1 - y_hi) * 2 + (leaf >> 2)]
                for h in range(2):
                    columns = pl.ds(h * BLK, BLK)
                    for source, target in (
                        (arrays[4].at[pl.ds(0, BLK), columns], to.at[16 + h]),
                        (arrays[4].at[pl.ds(BLK, 64), columns], to.at[18, pl.ds(h * 64, 64)]),
                    ):
                        d = copy(source, target, sem)
                        d.wait() if wait else d.start()

    arrays = arrays if extra is None else arrays + [extra]
    return call(body, [tab] + arrays, [(4, 16 if extra is None else 19, BLK, BLK)], "pack_y")[0]


def pack_z(c, tab, array, extra=None):
    def body(ins, held, sem):
        tab, array = ins[:2]
        leaf, front = tab[0], tab[1]
        z, y_lo = leaf & 3, leaf >> 2
        for wait in (False, True):
            for source in range(4):
                from_lo = source & 1
                group = from_lo * 4 + z

                @pl.when(tab[T_M + group * 16 + front] > c)
                def _():
                    def one(s, carry):
                        i = group * UB + (source >> 1) * 16 + s
                        owner = tab[T_R + i]

                        @pl.when((owner >> 2) == y_lo)
                        def _():
                            d = copy(array.at[source, s], held.at[(owner - z) & 3, from_lo, tab[T_RANK + i]], sem)
                            d.wait() if wait else d.start()

                        return carry

                    lax.fori_loop(0, 16, one, 0)

            if extra is not None:
                for k in range(4):
                    for h in range(2):
                        d = copy(ins[2].at[:, pl.ds(h * BLK, BLK)], held.at[k, h, 8], sem)
                        d.wait() if wait else d.start()

    more = [] if extra is None else [extra]
    return call(body, [tab, array] + more, [(2, 8 + len(more), BLK, BLK)] * 4, "pack_z")


def pack_panel(meta, child, front_tile):
    def body(ins, held, sem):
        meta, child, tile = ins
        leaf, front = meta[UB], meta[UB + 1]
        for wait in (False, True):
            def go(source, at):
                d = copy(source, held.at[(0,) + at], sem)
                d.wait() if wait else d.start()

            for j in range(NPAN):
                @pl.when(meta[j] < NPAN)
                def _():
                    for r in range(2):
                        go(child.at[r, :, pl.ds(j * BLK, BLK)], (meta[front * 2 + r] >> 4, r * NPAN + meta[j]))

            @pl.when((front == 0) & (meta[0] == 0) & (meta[1] == 1))
            def _():
                for t in range(8):
                    go(child.at[1, :, pl.ds(0, BLK)], (t, 4))

            @pl.when((front == 0) & (leaf == 0))
            def _():
                for t in range(8):
                    go(tile.at[pl.ds(BLK, BLK), pl.ds(0, BLK)], (t, 5))

    return call(body, [meta, child, front_tile], [(8, 6, BLK, BLK)], "pack_panel")[0]


def panel_part(flat, front_tile, arrived):
    def kernel(flat, tile, arrived, o0, o1, o2, o3, total, held, sem, tile_sem):
        leaf, front = flat[256], flat[257]
        y_hi, x, core = front >> 3, (front >> 1) & 3, front & 1
        come = copy(arrived, held, sem)
        come.start()

        def place(u):
            return (((u >> 1) & 3) - x) & 3, pl.ds(pl.multiple_of((((u & 1) ^ core) * 2 + ((u >> 3) ^ y_hi)) * BLK, BLK), BLK)

        def rows(act):
            def one(u, carry):
                act(copy(tile.at[pl.ds(pl.multiple_of(u * BLK, BLK), BLK), pl.ds(0, NPAN * BLK)], total.at[place(u)], tile_sem))
                return carry

            lax.fori_loop(0, 16, one, 0)

        @pl.when(front == 0)
        def _():
            rows(lambda d: d.start())
            rows(lambda d: d.wait())

        @pl.when(front != 0)
        def _():
            total[...] = jnp.zeros_like(total)

        come.wait()

        @pl.when(front == 0)
        def _():
            for k in range(4):
                for h in range(2):
                    total[k, pl.ds(512, 64), pl.ds(h * BLK, BLK)] = held[0, 5, pl.ds(h * 64, 64)]

            def corner(g, carry):
                @pl.when((flat[g * UB] == 0) & (flat[g * UB + 1] == 1))
                def _():
                    for k in range(4):
                        for h in range(2):
                            total[k, pl.ds(512, 64), pl.ds(h * BLK, BLK)] += held[g, 4, pl.ds(h * 64, 64)]

                return carry

            lax.fori_loop(0, 8, corner, 0)

        def add(n, carry):
            g, r = n >> 1, n & 1
            parent = flat[g * UB + front * 2 + r]

            @pl.when((parent >> 4) == leaf)
            def _():
                k, at = place(parent & 15)
                for v in range(NPAN):
                    @pl.when((flat[g * UB] == v) | (flat[g * UB + 1] == v))
                    def _():
                        total[k, at, pl.ds(v * BLK, BLK)] += held[g, r * NPAN + v]

            return carry

        lax.fori_loop(0, 16, add, 0)
        out = [copy(total.at[k], o, sem) for k, o in enumerate((o0, o1, o2, o3))]
        for o in out:
            o.start()
        for o in out:
            o.wait()

    block = (4 * BLK + 64, NPAN * BLK)
    return pl.pallas_call(
        kernel,
        out_shape=[jax.ShapeDtypeStruct(block, jnp.float32)] * 4,
        in_specs=[SMEM, HBM, HBM],
        out_specs=[HBM] * 4,
        scratch_shapes=[
            pltpu.VMEM((4,) + block, jnp.float32),
            pltpu.VMEM((8, 6, BLK, BLK), jnp.float32),
            pltpu.SemaphoreType.DMA(()),
            pltpu.SemaphoreType.DMA(()),
        ],
        compiler_params=pltpu.CompilerParams(vmem_limit_bytes=VMEM),
        cost_estimate=COST,
        name="panel_part",
    )(flat, front_tile, arrived)


def product(a, b, precision=lax.Precision.HIGHEST):
    return lax.dot_general(a, b, (((1,), (1,)), ((), ())), precision=precision, preferred_element_type=jnp.float32)


def factors(tab, block_inv, corner, sources, sides, of_rows):
    n = len(sources)
    blocks = 8

    def kernel(tab, inv, corner, *refs):
        sources, outs = refs[:n], refs[n:]
        leaf, front = tab[0], tab[1]
        below = product(corner[...], inv[0])
        for side, source in zip(sides, sources):
            for k in range(4):
                for m in range(2 if of_rows else 1):
                    if of_rows:
                        at = ((front >> 3) ^ side) * 8 + (((front >> 1) - k) & 3) * 2 + ((front & 1) ^ m)
                        raw = source[k, m]
                    else:
                        at = ((leaf >> 2) ^ side) * 4 + ((leaf - k) & 3)
                        raw = source[k]
                    first = ((leaf if of_rows else front) == 0) & (at == 0)
                    one = product(raw[:, :BLK], inv[0])
                    two = product(raw[:, BLK:] - product(one, below), inv[1])
                    two = jnp.where(first, 0.0, two)
                    rows = pl.ds(pl.multiple_of((at & 7) * BLK, BLK), BLK)
                    for h, part in enumerate((one, two)):
                        high = part.astype(jnp.bfloat16)
                        low = (part - high.astype(jnp.float32)).astype(jnp.bfloat16)
                        for t, value in enumerate((high, low, high) if of_rows else (high, high, low)):
                            outs[0][rows, pl.ds((t * 2 + h) * BLK, BLK)] = value
                        if of_rows:
                            outs[1][rows, pl.ds(h * BLK, BLK)] = part

    vmem = pl.BlockSpec(memory_space=pltpu.VMEM)
    shapes = [jax.ShapeDtypeStruct((blocks * BLK, 6 * BLK), jnp.bfloat16)]
    if of_rows:
        shapes.append(jax.ShapeDtypeStruct((blocks * BLK, 2 * BLK), jnp.float32))
    return pl.pallas_call(
        kernel,
        out_shape=shapes,
        in_specs=[SMEM] + [vmem] * (2 + n),
        out_specs=[vmem] * len(shapes),
        compiler_params=pltpu.CompilerParams(vmem_limit_bytes=VMEM),
        cost_estimate=COST,
        name="factors",
    )(tab, block_inv, corner, *sources)


def accumulate(chunks, tab, tile, arrays, panel=None):
    n_arrays = 4 * len(chunks)
    width = tile.shape[1]
    ranks = sorted({c for c, _, _ in chunks})
    steps = tile.shape[0] // (BLK * STEP)
    half = steps // 2

    def kernel(tab, tile, *refs):
        arrays, refs = refs[:n_arrays], refs[n_arrays:]
        if panel is not None:
            (near, near_plain, far, far_plain, right), refs = refs[:5], refs[5:]
        out, held, sems = refs
        i = pl.program_id(0)
        z = tab[0] & 3

        def each(step, act):
            for r in range(STEP):
                for g in range(8):
                    group = g // 4 * 4 + ((z - g) & 3)
                    p = tab[T_PROW + group * 16 + step * STEP + r]

                    @pl.when(p >= 0)
                    def _():
                        for m, c in enumerate(ranks):
                            v = tab[T_VCOL + group * 4 + c]

                            @pl.when(v >= 0)
                            def _():
                                act(r, g, p, m, c, v)

        def fetch(step, wait):
            slot = step & 1

            def act(r, g, p, m, c, v):
                for n, (cc, off, rows) in enumerate(chunks):
                    if cc == c:
                        source = arrays[n * 4 + g % 4].at[g // 4, p]
                        one = copy(source, held.at[slot, r, g, m, pl.ds(off, rows)], sems.at[slot])
                        one.wait() if wait else one.start()

            each(step, act)

        @pl.when(i == 0)
        def _():
            fetch(0, False)

        @pl.when(i + 1 < steps)
        def _():
            fetch(i + 1, False)

        if panel is None:
            out[...] = tile[...]
        else:
            mine = (i // half) == (tab[1] >> 3)
            out[...] = tile[...] - product(jnp.where(mine, near[...], far[...]), right[...], None)
        fetch(i, True)
        slot = i & 1

        def add(r, g, p, m, c, v):
            out[pl.ds(r * BLK, BLK), pl.ds(pl.multiple_of(v * BLK, BLK), BLK)] += held[slot, r, g, m]

        each(i, add)
        if panel is not None:
            @pl.when(tab[1] == 0)
            def _():
                out[:, pl.ds(0, 2 * BLK)] = jnp.where(mine, near_plain[...], far_plain[...])

    rows = BLK * STEP
    specs = [SMEM, pl.BlockSpec((rows, width), lambda i: (i, 0))] + [HBM] * n_arrays
    operands = [tab, tile] + list(arrays)
    if panel is not None:
        specs += [
            pl.BlockSpec((rows, 6 * BLK), lambda i: (i % half, 0)),
            pl.BlockSpec((rows, 2 * BLK), lambda i: (i % half, 0)),
        ] * 2 + [pl.BlockSpec((width, 6 * BLK), lambda i: (0, 0))]
        operands += list(panel)
    return pl.pallas_call(
        kernel,
        out_shape=jax.ShapeDtypeStruct(tile.shape, jnp.float32),
        grid=(steps,),
        in_specs=specs,
        out_specs=pl.BlockSpec((rows, width), lambda i: (i, 0)),
        scratch_shapes=[
            pltpu.VMEM((2, STEP, 8, len(ranks), BLK, BLK), jnp.float32),
            pltpu.SemaphoreType.DMA((2,)),
        ],
        compiler_params=pltpu.CompilerParams(vmem_limit_bytes=VMEM),
        cost_estimate=COST,
        name="accumulate" if panel is None else "final",
    )(*operands)


def shift_x(a, dx, dc):
    pairs = [
        (front_at(h, x, c), front_at(h, x + dx, c + dc)) for h in range(2) for x in range(4) for c in range(2)
    ]
    return lax.ppermute(a, "front", pairs)


def exchange_y(a):
    groups = [
        [device_at(leaf_at(y, z), front_at(y // 2, x, c)) for y in range(4)]
        for z in range(4) for x in range(4) for c in range(2)
    ]
    return lax.all_to_all(a, ("leaf", "front"), 0, 0, axis_index_groups=groups, tiled=True)


def shift_z(a, dz):
    return lax.ppermute(a, "leaf", [(leaf_at(l, z), leaf_at(l, z + dz)) for l in range(2) for z in range(4)])


def tie(values, *after):
    return list(lax.optimization_barrier(tuple(values) + after)[:len(values)])


def other_device(a, bit):
    return lax.ppermute(a, ("leaf", "front"), [(d, d ^ bit) for d in range(128)])


OTHER_CORE, OTHER_Y_HI, OTHER_Y_LO = 1, 8, 64


def tables(assembly, leaf, front):
    col_owner, row_owner = assembly >> 3, assembly >> 4
    earlier = jnp.arange(UB)[:, None] > jnp.arange(UB)[None, :]

    def rank(owner):
        same = (owner[:, :, None] == owner[:, None, :]) & earlier[None]
        return jnp.sum(same.astype(jnp.int32), axis=2)

    def pick(match, value):
        return jnp.sum(jnp.where(match, value + 1, 0), axis=1).astype(jnp.int32) - 1

    row_rank, col_rank = rank(row_owner), rank(col_owner)
    count = jnp.sum((col_owner[:, :, None] == jnp.arange(16)).astype(jnp.int32), axis=1)
    mine = row_owner == leaf
    row_u = pick(
        mine[:, :, None] & (row_rank[:, :, None] == jnp.arange(8)), (assembly & 15)[:, :, None]
    )
    row_p = pick(assembly[:, :, None] == leaf * 16 + jnp.arange(16), row_rank[:, :, None])
    col_v = pick(
        (col_owner == front)[:, :, None] & (col_rank[:, :, None] == jnp.arange(CAPF)), (assembly & 7)[:, :, None]
    )
    head = jnp.concatenate([leaf[None], front[None], jnp.zeros((T_R - 2,), jnp.int32)])
    parts = [head] + [t.reshape(-1) for t in (row_owner, row_rank, count, row_u, row_p, col_v)]
    size = sum(t.shape[0] for t in parts)
    return jnp.concatenate(parts + [jnp.zeros((T_ALL - size,), jnp.int32)])


def per_device(child_update, assembly, front_matrix, block_inv):
    leaf, front = lax.axis_index("leaf"), lax.axis_index("front")
    child = child_update.reshape(2, BLK, child_update.shape[2])
    own = lax.dynamic_index_in_dim(assembly, leaf, 0, keepdims=False)
    count = jnp.sum(((own >> 3)[:, None] == jnp.arange(16)).astype(jnp.int32), axis=0)
    meta = jnp.concatenate([own, leaf[None], front[None], jnp.zeros((COUNT - UB - 2,), jnp.int32), count])
    tab = tables(assembly, leaf, front)

    flat = jnp.concatenate([assembly.reshape(-1), leaf[None], front[None], jnp.zeros((126,), jnp.int32)])
    n = CAPF

    arrived = lax.all_to_all(pack_panel(meta, child, front_matrix), "leaf", 0, 0, tiled=True)
    first = shift_x(pack_core(0, 1, meta, child)[0], 0, 1)
    rest = shift_x(pack_core(1, n, meta, child)[0], 0, 1)

    outs = pack_x(0, 1, meta, child, first, 0, [])
    x_in = [[outs[0]] + [shift_x(outs[k], k, 0) for k in range(1, 4)]]
    outs = pack_x(1, 2, meta, child, rest, 1, x_in[0][1:])
    x_in.append([outs[0]] + [shift_x(outs[k], k, 0) for k in range(1, 4)])
    parts = panel_part(tie([flat], outs[0])[0], front_matrix, arrived)
    parts = [parts[0]] + [shift_x(a, k + 1, 0) for k, a in enumerate(tie(parts[1:], x_in[1][1], x_in[1][3]))]
    outs = pack_x(2, n, meta, child, rest, 1, x_in[1][1:] + parts[1:])
    x_in.append([outs[0]] + [shift_x(outs[k], k, 0) for k in range(1, 4)])
    *parts, x_in[1][2] = tie(parts + [x_in[1][2]])
    part = parts[0] + parts[1] + parts[2] + parts[3]
    part = jnp.concatenate([part[:256], part[512:]]) + other_device(part[256:], OTHER_CORE)
    kept = jnp.concatenate([part[:BLK], part[256:]])
    sent = part[BLK:]
    bases = (0, 1, 2, 2)
    y_in, z_out, z_in, gates = [], [], [], [[arrived], [], [], [], []]

    for s in range(n):
        packed = pack_y(s, tab, x_in[min(s, 2)], bases[s], sent if s == 1 else None)
        before = ([y_in[s - 1]] if s else []) + (z_in[s - 2][1:] if s > 1 else []) + gates[s]
        y_in.append(exchange_y(tie([packed], *before)[0]))
        if s == 1:
            got = lax.dynamic_index_in_dim(y_in[1][:, 16:], (1 - (front >> 3)) * 2 + (leaf >> 2), 0, keepdims=False)
            corner = jnp.concatenate([kept[BLK:, :BLK], kept[BLK:, BLK:]]) + got[2]
            part = kept[:BLK] + jnp.concatenate([got[0], got[1]], axis=1)
            near = jnp.stack([part, other_device(part, OTHER_CORE)])
            near = jnp.stack([near] + [shift_x(near, k, 0) for k in range(1, 4)])
            pairs = [(b, device_at(b % 8, b // 8)) for b in range(128)]
            moved = lax.ppermute(part, ("leaf", "front"), pairs)
            gates[3] += [near, moved]
        before = z_in[s - 1][1:] if s else []
        z_out.append(pack_z(s, tab, tie([y_in[s]], *before)[0] if before else y_in[s], moved if s == 2 else None))
        z_in.append([z_out[s][0]] + [shift_z(z_out[s][k], k) for k in range(1, 4)])

    columns_near = jnp.stack([jnp.concatenate([z_in[2][k][0, 8], z_in[2][k][1, 8]], axis=1) for k in range(4)])
    near_late, columns_late = tie([near, columns_near], z_out[n - 1][0])
    far = other_device(near_late, OTHER_Y_HI)
    columns_far = other_device(columns_late, OTHER_Y_LO)
    left = factors(tab, block_inv, corner, [near], [0], True)
    tile = accumulate(WHOLE[:3], tab, front_matrix, z_in[0] + z_in[1] + z_in[2])
    left = left + factors(tab, block_inv, corner, [far], [1], True)
    columns_far = tie([columns_far], left[2], tile)[0]
    right = factors(tab, block_inv, corner, [columns_near, columns_far], [0, 1], False)
    return accumulate(WHOLE[3:], tab, tile, z_in[3], left + right)


def solution(mesh):
    placed = (P("leaf", "front", None), P(), P("leaf", "front"), P())
    return jax.shard_map(
        per_device, mesh=mesh, in_specs=placed, out_specs=P("leaf", "front"), check_vma=False
    )
```

```python
import functools

import jax
import jax.numpy as jnp
from jax import lax
from jax.experimental import pallas as pl
from jax.experimental.pallas import tpu as pltpu
from jax.sharding import PartitionSpec as P

BLK = 128
CAPF = 4
NPAN = 2
UB = 32
WHOLE = [(c, 0, 128) for c in range(CAPF)]
COUNT = 48

T_R, T_RANK, T_M, T_ROWU, T_PROW, T_VCOL, T_ALL = 128, 384, 640, 768, 832, 960, 1024

HBM = pl.BlockSpec(memory_space=pltpu.HBM)
SMEM = pl.BlockSpec(memory_space=pltpu.SMEM)
COST = pl.CostEstimate(flops=1000, bytes_accessed=1 << 16, transcendentals=0)
VMEM = 60 << 20
STEP = 2


def leaf_at(y_lo, z):
    return y_lo % 2 * 4 + z % 4


def front_at(y_hi, x, core):
    return y_hi % 2 * 8 + x % 4 * 2 + core % 2


def device_at(leaf, front):
    return leaf * 16 + front


def copy(src, dst, sem):
    return pltpu.make_async_copy(src, dst, sem)


def call(body, operands, outs, name):
    n = len(outs)

    def kernel(*refs):
        ins, results, held, sem = refs[:-n - 2], refs[-n - 2:-2], refs[-2], refs[-1]
        body(ins, held, sem)
        writes = [copy(held.at[k], results[k], sem) for k in range(n)]
        for w in writes:
            w.start()
        for w in writes:
            w.wait()

    return pl.pallas_call(
        kernel,
        out_shape=[jax.ShapeDtypeStruct(s, jnp.float32) for s in outs],
        in_specs=[SMEM] + [HBM] * (len(operands) - 1),
        out_specs=[HBM] * n,
        scratch_shapes=[pltpu.VMEM((n,) + outs[0], jnp.float32), pltpu.SemaphoreType.DMA(())],
        compiler_params=pltpu.CompilerParams(vmem_limit_bytes=VMEM),
        cost_estimate=COST,
        name=name,
    )(*operands)


def own_columns(meta, act):
    def column(j, carry):
        before, rank = carry
        owner = meta[j] >> 3
        rank = jnp.where(owner == before, rank + 1, 0)
        act(j, owner, rank)
        return owner, rank

    lax.fori_loop(0, UB, column, (jnp.int32(-1), jnp.int32(0)))


def pack_core(first, last, meta, child):
    def body(ins, held, sem):
        meta, child = ins[:2]
        core = meta[UB + 1] & 1
        for wait in (False, True):
            def act(j, owner, rank, wait=wait):
                @pl.when((rank >= first) & (rank < last) & ((owner & 1) != core))
                def _():
                    columns = pl.ds(pl.multiple_of(j * BLK, BLK), BLK)
                    one = copy(child.at[:, :, columns], held.at[0, rank - first, owner >> 1], sem)
                    one.wait() if wait else one.start()

            own_columns(meta, act)

    return call(body, [meta, child], [(last - first, 8, 2, BLK, BLK)], "pack_core")


def pack_x(first, last, meta, child, crossed, base, after):
    def body(ins, held, sem):
        meta, child, crossed = ins[:3]
        front = meta[UB + 1]
        x, core = (front >> 1) & 3, front & 1
        for wait in (False, True):
            def act(j, owner, rank, wait=wait):
                @pl.when((rank >= first) & (rank < last) & ((owner & 1) == core))
                def _():
                    source = child.at[:, :, pl.ds(pl.multiple_of(j * BLK, BLK), BLK)]
                    d = copy(source, held.at[((owner >> 1) - x) & 3, rank - first, owner >> 3, 0], sem)
                    d.wait() if wait else d.start()

            def other(f, carry, wait=wait):
                for rank in range(first, last):
                    @pl.when(meta[COUNT + f * 2 + core] > rank)
                    def _():
                        d = copy(crossed.at[rank - base, f], held.at[(f - x) & 3, rank - first, f >> 2, 1], sem)
                        d.wait() if wait else d.start()

                return carry

            own_columns(meta, act)
            lax.fori_loop(0, 8, other, 0)

    return call(body, [meta, child, crossed] + after, [(last - first, 2, 2, 2, BLK, BLK)] * 4, "pack_x")


def pack_y(c, tab, arrays, base, extra=None):
    def body(ins, held, sem):
        tab, arrays = ins[0], ins[1:]
        leaf, front = tab[0], tab[1]
        y_hi, x, core = front >> 3, (front >> 1) & 3, front & 1
        for wait in (False, True):
            for to_hi in range(2):
                @pl.when(tab[T_M + leaf * 16 + to_hi * 8 + (front & 7)] > c)
                def _():
                    for k in range(4):
                        def one(n, carry):
                            other, r = n >> 1, n & 1
                            slot = (((x - k) & 3) * 2 + (core ^ other)) * 2 + r
                            owner = tab[T_R + leaf * UB + y_hi * 16 + slot]
                            d = copy(arrays[k].at[c - base, to_hi, other, r], held.at[0, to_hi * 2 + (owner >> 2), slot], sem)
                            d.wait() if wait else d.start()
                            return carry

                        lax.fori_loop(0, 4, one, 0)

            if extra is not None:
                to = held.at[0, (1 - y_hi) * 2 + (leaf >> 2)]
                for h in range(2):
                    columns = pl.ds(h * BLK, BLK)
                    for source, target in (
                        (arrays[4].at[pl.ds(0, BLK), columns], to.at[16 + h]),
                        (arrays[4].at[pl.ds(BLK, 64), columns], to.at[18, pl.ds(h * 64, 64)]),
                    ):
                        d = copy(source, target, sem)
                        d.wait() if wait else d.start()

    arrays = arrays if extra is None else arrays + [extra]
    return call(body, [tab] + arrays, [(4, 16 if extra is None else 19, BLK, BLK)], "pack_y")[0]


def pack_z(c, tab, array, extra=None):
    def body(ins, held, sem):
        tab, array = ins[:2]
        leaf, front = tab[0], tab[1]
        z, y_lo = leaf & 3, leaf >> 2
        for wait in (False, True):
            for source in range(4):
                from_lo = source & 1
                group = from_lo * 4 + z

                @pl.when(tab[T_M + group * 16 + front] > c)
                def _():
                    def one(s, carry):
                        i = group * UB + (source >> 1) * 16 + s
                        owner = tab[T_R + i]

                        @pl.when((owner >> 2) == y_lo)
                        def _():
                            d = copy(array.at[source, s], held.at[(owner - z) & 3, from_lo, tab[T_RANK + i]], sem)
                            d.wait() if wait else d.start()

                        return carry

                    lax.fori_loop(0, 16, one, 0)

            if extra is not None:
                for k in range(4):
                    for h in range(2):
                        d = copy(ins[2].at[:, pl.ds(h * BLK, BLK)], held.at[k, h, 8], sem)
                        d.wait() if wait else d.start()

    more = [] if extra is None else [extra]
    return call(body, [tab, array] + more, [(2, 8 + len(more), BLK, BLK)] * 4, "pack_z")


def pack_panel(meta, child, front_tile):
    def body(ins, held, sem):
        meta, child, tile = ins
        leaf, front = meta[UB], meta[UB + 1]
        for wait in (False, True):
            def go(source, at):
                d = copy(source, held.at[(0,) + at], sem)
                d.wait() if wait else d.start()

            for j in range(NPAN):
                @pl.when(meta[j] < NPAN)
                def _():
                    for r in range(2):
                        go(child.at[r, :, pl.ds(j * BLK, BLK)], (meta[front * 2 + r] >> 4, r * NPAN + meta[j]))

            @pl.when((front == 0) & (meta[0] == 0) & (meta[1] == 1))
            def _():
                for t in range(8):
                    go(child.at[1, :, pl.ds(0, BLK)], (t, 4))

            @pl.when((front == 0) & (leaf == 0))
            def _():
                for t in range(8):
                    go(tile.at[pl.ds(BLK, BLK), pl.ds(0, BLK)], (t, 5))

    return call(body, [meta, child, front_tile], [(8, 6, BLK, BLK)], "pack_panel")[0]


def panel_part(flat, front_tile, arrived):
    def kernel(flat, tile, arrived, o0, o1, total, held, sem, tile_sem):
        leaf, front = flat[256], flat[257]
        y_hi, x, core = front >> 3, (front >> 1) & 3, front & 1
        come = copy(arrived, held, sem)
        come.start()

        def place(u):
            return (u & 1) ^ core, (((u >> 1) & 3) - x) & 3, pl.ds(pl.multiple_of(((u >> 3) ^ y_hi) * BLK, BLK), BLK)

        def rows(act):
            def one(u, carry):
                act(copy(tile.at[pl.ds(pl.multiple_of(u * BLK, BLK), BLK), pl.ds(0, NPAN * BLK)], total.at[place(u)], tile_sem))
                return carry

            lax.fori_loop(0, 16, one, 0)

        @pl.when(front == 0)
        def _():
            rows(lambda d: d.start())
            rows(lambda d: d.wait())

        @pl.when(front != 0)
        def _():
            total[...] = jnp.zeros_like(total)

        come.wait()

        @pl.when(front == 0)
        def _():
            for k in range(8):
                for h in range(2):
                    total[k // 4, k % 4, pl.ds(256, 64), pl.ds(h * BLK, BLK)] = held[0, 5, pl.ds(h * 64, 64)]

            def corner(g, carry):
                @pl.when((flat[g * UB] == 0) & (flat[g * UB + 1] == 1))
                def _():
                    for k in range(8):
                        for h in range(2):
                            total[k // 4, k % 4, pl.ds(256, 64), pl.ds(h * BLK, BLK)] += held[g, 4, pl.ds(h * 64, 64)]

                return carry

            lax.fori_loop(0, 8, corner, 0)

        def add(n, carry):
            g, r = n >> 1, n & 1
            parent = flat[g * UB + front * 2 + r]

            @pl.when((parent >> 4) == leaf)
            def _():
                other, k, at = place(parent & 15)
                for v in range(NPAN):
                    @pl.when((flat[g * UB] == v) | (flat[g * UB + 1] == v))
                    def _():
                        total[other, k, at, pl.ds(v * BLK, BLK)] += held[g, r * NPAN + v]

            return carry

        lax.fori_loop(0, 16, add, 0)
        out = [copy(total.at[k], o, sem) for k, o in enumerate((o0, o1))]
        for o in out:
            o.start()
        for o in out:
            o.wait()

    block = (4, 2 * BLK + 64, NPAN * BLK)
    return pl.pallas_call(
        kernel,
        out_shape=[jax.ShapeDtypeStruct(block, jnp.float32)] * 2,
        in_specs=[SMEM, HBM, HBM],
        out_specs=[HBM] * 2,
        scratch_shapes=[
            pltpu.VMEM((2,) + block, jnp.float32),
            pltpu.VMEM((8, 6, BLK, BLK), jnp.float32),
            pltpu.SemaphoreType.DMA(()),
            pltpu.SemaphoreType.DMA(()),
        ],
        compiler_params=pltpu.CompilerParams(vmem_limit_bytes=VMEM),
        cost_estimate=COST,
        name="panel_part",
    )(flat, front_tile, arrived)


def product(a, b, precision=lax.Precision.HIGHEST):
    return lax.dot_general(a, b, (((1,), (1,)), ((), ())), precision=precision, preferred_element_type=jnp.float32)


def factors(tab, block_inv, corner, sources, sides, of_rows):
    n = len(sources)
    blocks = 8

    def kernel(tab, inv, corner, *refs):
        sources, outs = refs[:n], refs[n:]
        leaf, front = tab[0], tab[1]
        below = product(corner[...], inv[0])
        for side, source in zip(sides, sources):
            for k in range(4):
                for m in range(2 if of_rows else 1):
                    if of_rows:
                        at = ((front >> 3) ^ side) * 8 + (((front >> 1) - k) & 3) * 2 + ((front & 1) ^ m)
                        raw = source[k, m]
                    else:
                        at = ((leaf >> 2) ^ side) * 4 + ((leaf - k) & 3)
                        raw = source[k]
                    first = ((leaf if of_rows else front) == 0) & (at == 0)
                    one = product(raw[:, :BLK], inv[0])
                    two = product(raw[:, BLK:] - product(one, below), inv[1])
                    two = jnp.where(first, 0.0, two)
                    rows = pl.ds(pl.multiple_of((at & 7) * BLK, BLK), BLK)
                    for h, part in enumerate((one, two)):
                        high = part.astype(jnp.bfloat16)
                        low = (part - high.astype(jnp.float32)).astype(jnp.bfloat16)
                        for t, value in enumerate((high, low, high) if of_rows else (high, high, low)):
                            outs[0][rows, pl.ds((t * 2 + h) * BLK, BLK)] = value
                        if of_rows:
                            outs[1][rows, pl.ds(h * BLK, BLK)] = part

    vmem = pl.BlockSpec(memory_space=pltpu.VMEM)
    shapes = [jax.ShapeDtypeStruct((blocks * BLK, 6 * BLK), jnp.bfloat16)]
    if of_rows:
        shapes.append(jax.ShapeDtypeStruct((blocks * BLK, 2 * BLK), jnp.float32))
    return pl.pallas_call(
        kernel,
        out_shape=shapes,
        in_specs=[SMEM] + [vmem] * (2 + n),
        out_specs=[vmem] * len(shapes),
        compiler_params=pltpu.CompilerParams(vmem_limit_bytes=VMEM),
        cost_estimate=COST,
        name="factors",
    )(tab, block_inv, corner, *sources)


def accumulate(chunks, tab, tile, arrays, panel=None):
    n_arrays = 4 * len(chunks)
    width = tile.shape[1]
    ranks = sorted({c for c, _, _ in chunks})
    steps = tile.shape[0] // (BLK * STEP)
    half = steps // 2

    def kernel(tab, tile, *refs):
        arrays, refs = refs[:n_arrays], refs[n_arrays:]
        if panel is not None:
            (near, near_plain, far, far_plain, right), refs = refs[:5], refs[5:]
        out, held, sems = refs
        i = pl.program_id(0)
        z = tab[0] & 3

        def each(step, act):
            for r in range(STEP):
                for g in range(8):
                    group = g // 4 * 4 + ((z - g) & 3)
                    p = tab[T_PROW + group * 16 + step * STEP + r]

                    @pl.when(p >= 0)
                    def _():
                        for m, c in enumerate(ranks):
                            v = tab[T_VCOL + group * 4 + c]

                            @pl.when(v >= 0)
                            def _():
                                act(r, g, p, m, c, v)

        def fetch(step, wait):
            slot = step & 1

            def act(r, g, p, m, c, v):
                for n, (cc, off, rows) in enumerate(chunks):
                    if cc == c:
                        source = arrays[n * 4 + g % 4].at[g // 4, p]
                        one = copy(source, held.at[slot, r, g, m, pl.ds(off, rows)], sems.at[slot])
                        one.wait() if wait else one.start()

            each(step, act)

        @pl.when(i == 0)
        def _():
            fetch(0, False)

        @pl.when(i + 1 < steps)
        def _():
            fetch(i + 1, False)

        if panel is None:
            out[...] = tile[...]
        else:
            mine = (i // half) == (tab[1] >> 3)
            out[...] = tile[...] - product(jnp.where(mine, near[...], far[...]), right[...], None)
        fetch(i, True)
        slot = i & 1

        def add(r, g, p, m, c, v):
            out[pl.ds(r * BLK, BLK), pl.ds(pl.multiple_of(v * BLK, BLK), BLK)] += held[slot, r, g, m]

        each(i, add)
        if panel is not None:
            @pl.when(tab[1] == 0)
            def _():
                out[:, pl.ds(0, 2 * BLK)] = jnp.where(mine, near_plain[...], far_plain[...])

    rows = BLK * STEP
    specs = [SMEM, pl.BlockSpec((rows, width), lambda i: (i, 0))] + [HBM] * n_arrays
    operands = [tab, tile] + list(arrays)
    if panel is not None:
        specs += [
            pl.BlockSpec((rows, 6 * BLK), lambda i: (i % half, 0)),
            pl.BlockSpec((rows, 2 * BLK), lambda i: (i % half, 0)),
        ] * 2 + [pl.BlockSpec((width, 6 * BLK), lambda i: (0, 0))]
        operands += list(panel)
    return pl.pallas_call(
        kernel,
        out_shape=jax.ShapeDtypeStruct(tile.shape, jnp.float32),
        grid=(steps,),
        in_specs=specs,
        out_specs=pl.BlockSpec((rows, width), lambda i: (i, 0)),
        scratch_shapes=[
            pltpu.VMEM((2, STEP, 8, len(ranks), BLK, BLK), jnp.float32),
            pltpu.SemaphoreType.DMA((2,)),
        ],
        compiler_params=pltpu.CompilerParams(vmem_limit_bytes=VMEM),
        cost_estimate=COST,
        name="accumulate" if panel is None else "final",
    )(*operands)


def shift_x(a, dx, dc):
    pairs = [
        (front_at(h, x, c), front_at(h, x + dx, c + dc)) for h in range(2) for x in range(4) for c in range(2)
    ]
    return lax.ppermute(a, "front", pairs)


def exchange_y(a):
    groups = [
        [device_at(leaf_at(y, z), front_at(y // 2, x, c)) for y in range(4)]
        for z in range(4) for x in range(4) for c in range(2)
    ]
    return lax.all_to_all(a, ("leaf", "front"), 0, 0, axis_index_groups=groups, tiled=True)


def shift_z(a, dz):
    return lax.ppermute(a, "leaf", [(leaf_at(l, z), leaf_at(l, z + dz)) for l in range(2) for z in range(4)])


def tie(values, *after):
    return list(lax.optimization_barrier(tuple(values) + after)[:len(values)])


def other_device(a, bit):
    return lax.ppermute(a, ("leaf", "front"), [(d, d ^ bit) for d in range(128)])


OTHER_CORE, OTHER_Y_HI, OTHER_Y_LO = 1, 8, 64


def tables(assembly, leaf, front):
    col_owner, row_owner = assembly >> 3, assembly >> 4
    earlier = jnp.arange(UB)[:, None] > jnp.arange(UB)[None, :]

    def rank(owner):
        same = (owner[:, :, None] == owner[:, None, :]) & earlier[None]
        return jnp.sum(same.astype(jnp.int32), axis=2)

    def pick(match, value):
        return jnp.sum(jnp.where(match, value + 1, 0), axis=1).astype(jnp.int32) - 1

    row_rank, col_rank = rank(row_owner), rank(col_owner)
    count = jnp.sum((col_owner[:, :, None] == jnp.arange(16)).astype(jnp.int32), axis=1)
    mine = row_owner == leaf
    row_u = pick(
        mine[:, :, None] & (row_rank[:, :, None] == jnp.arange(8)), (assembly & 15)[:, :, None]
    )
    row_p = pick(assembly[:, :, None] == leaf * 16 + jnp.arange(16), row_rank[:, :, None])
    col_v = pick(
        (col_owner == front)[:, :, None] & (col_rank[:, :, None] == jnp.arange(CAPF)), (assembly & 7)[:, :, None]
    )
    head = jnp.concatenate([leaf[None], front[None], jnp.zeros((T_R - 2,), jnp.int32)])
    parts = [head] + [t.reshape(-1) for t in (row_owner, row_rank, count, row_u, row_p, col_v)]
    size = sum(t.shape[0] for t in parts)
    return jnp.concatenate(parts + [jnp.zeros((T_ALL - size,), jnp.int32)])


def per_device(child_update, assembly, front_matrix, block_inv):
    leaf, front = lax.axis_index("leaf"), lax.axis_index("front")
    child = child_update.reshape(2, BLK, child_update.shape[2])
    own = lax.dynamic_index_in_dim(assembly, leaf, 0, keepdims=False)
    count = jnp.sum(((own >> 3)[:, None] == jnp.arange(16)).astype(jnp.int32), axis=0)
    meta = jnp.concatenate([own, leaf[None], front[None], jnp.zeros((COUNT - UB - 2,), jnp.int32), count])
    tab = tables(assembly, leaf, front)

    flat = jnp.concatenate([assembly.reshape(-1), leaf[None], front[None], jnp.zeros((126,), jnp.int32)])
    n = CAPF

    arrived = lax.all_to_all(pack_panel(meta, child, front_matrix), "leaf", 0, 0, tiled=True)
    first = shift_x(pack_core(0, 1, meta, child)[0], 0, 1)
    rest = shift_x(pack_core(1, n, meta, child)[0], 0, 1)

    outs = pack_x(0, 1, meta, child, first, 0, [])
    x_in = [[outs[0]] + [shift_x(outs[k], k, 0) for k in range(1, 4)]]
    outs = pack_x(1, 2, meta, child, rest, 1, x_in[0][1:])
    x_in.append([outs[0]] + [shift_x(outs[k], k, 0) for k in range(1, 4)])
    mine, others = panel_part(tie([flat], outs[0])[0], front_matrix, arrived)
    mine = mine + other_device(others, OTHER_CORE)
    parts = [mine[k] for k in range(4)]
    parts = [parts[0]] + [shift_x(a, k + 1, 0) for k, a in enumerate(tie(parts[1:], x_in[1][1], x_in[1][3]))]
    *parts, x_in[1][2] = tie(parts + [x_in[1][2]])
    outs = pack_x(2, n, meta, child, rest, 1, x_in[1][1:] + parts[1:])
    x_in.append([outs[0]] + [shift_x(outs[k], k, 0) for k in range(1, 4)])
    part = parts[0] + parts[1] + parts[2] + parts[3]
    kept = jnp.concatenate([part[:BLK], part[256:]])
    sent = part[BLK:]
    bases = (0, 1, 2, 2)
    y_in, z_out, z_in, gates = [], [], [], [[arrived], [], [], [], []]

    for s in range(n):
        if s == 1:
            sent = tie([sent], z_out[0][0])[0]
        packed = pack_y(s, tab, x_in[min(s, 2)], bases[s], sent if s == 1 else None)
        before = ([y_in[s - 1]] if s else []) + (z_in[s - 2][1:] if s > 1 else []) + gates[s]
        y_in.append(exchange_y(tie([packed], *before)[0]))
        if s == 1:
            got = lax.dynamic_index_in_dim(y_in[1][:, 16:], (1 - (front >> 3)) * 2 + (leaf >> 2), 0, keepdims=False)
            corner = jnp.concatenate([kept[BLK:, :BLK], kept[BLK:, BLK:]]) + got[2]
            part = kept[:BLK] + jnp.concatenate([got[0], got[1]], axis=1)
            near = jnp.stack([part, other_device(part, OTHER_CORE)])
            near = jnp.stack([near] + [shift_x(near, k, 0) for k in range(1, 4)])
            pairs = [(b, device_at(b % 8, b // 8)) for b in range(128)]
            moved = lax.ppermute(part, ("leaf", "front"), pairs)
            gates[3] += [near, moved]
        before = z_in[s - 1][1:] if s else []
        z_out.append(pack_z(s, tab, tie([y_in[s]], *before)[0] if before else y_in[s], moved if s == 2 else None))
        z_in.append([z_out[s][0]] + [shift_z(z_out[s][k], k) for k in range(1, 4)])

    columns_near = jnp.stack([jnp.concatenate([z_in[2][k][0, 8], z_in[2][k][1, 8]], axis=1) for k in range(4)])
    near_late, columns_late = tie([near, columns_near], z_out[n - 1][0])
    far = other_device(near_late, OTHER_Y_HI)
    columns_far = other_device(columns_late, OTHER_Y_LO)
    left = factors(tab, block_inv, corner, [near], [0], True)
    tile = accumulate(WHOLE[:3], tab, front_matrix, z_in[0] + z_in[1] + z_in[2])
    left = left + factors(tab, block_inv, corner, [far], [1], True)
    columns_far = tie([columns_far], left[2], tile)[0]
    right = factors(tab, block_inv, corner, [columns_near, columns_far], [0, 1], False)
    return accumulate(WHOLE[3:], tab, tile, z_in[3], left + right)


def solution(mesh):
    placed = (P("leaf", "front", None), P(), P("leaf", "front"), P())
    return jax.shard_map(
        per_device, mesh=mesh, in_specs=placed, out_specs=P("leaf", "front"), check_vma=False
    )
```

```python
import functools

import jax
import jax.numpy as jnp
from jax import lax
from jax.experimental import pallas as pl
from jax.experimental.pallas import tpu as pltpu
from jax.sharding import PartitionSpec as P

BLK = 128
CAPF = 4
NPAN = 2
UB = 32
WHOLE = [(c, 0, 128) for c in range(CAPF)]
COUNT = 48

T_R, T_RANK, T_M, T_ROWU, T_PROW, T_VCOL, T_ALL = 128, 384, 640, 768, 832, 960, 1024

HBM = pl.BlockSpec(memory_space=pltpu.HBM)
SMEM = pl.BlockSpec(memory_space=pltpu.SMEM)
COST = pl.CostEstimate(flops=1000, bytes_accessed=1 << 16, transcendentals=0)
VMEM = 60 << 20
STEP = 4


def leaf_at(y_lo, z):
    return y_lo % 2 * 4 + z % 4


def front_at(y_hi, x, core):
    return y_hi % 2 * 8 + x % 4 * 2 + core % 2


def device_at(leaf, front):
    return leaf * 16 + front


def copy(src, dst, sem):
    return pltpu.make_async_copy(src, dst, sem)


def call(body, operands, outs, name):
    n = len(outs)

    def kernel(*refs):
        ins, results, held, sem = refs[:-n - 2], refs[-n - 2:-2], refs[-2], refs[-1]
        body(ins, held, sem)
        writes = [copy(held.at[k], results[k], sem) for k in range(n)]
        for w in writes:
            w.start()
        for w in writes:
            w.wait()

    return pl.pallas_call(
        kernel,
        out_shape=[jax.ShapeDtypeStruct(s, jnp.float32) for s in outs],
        in_specs=[SMEM] + [HBM] * (len(operands) - 1),
        out_specs=[HBM] * n,
        scratch_shapes=[pltpu.VMEM((n,) + outs[0], jnp.float32), pltpu.SemaphoreType.DMA(())],
        compiler_params=pltpu.CompilerParams(vmem_limit_bytes=VMEM),
        cost_estimate=COST,
        name=name,
    )(*operands)


def own_columns(meta, act):
    def column(j, carry):
        before, rank = carry
        owner = meta[j] >> 3
        rank = jnp.where(owner == before, rank + 1, 0)
        act(j, owner, rank)
        return owner, rank

    lax.fori_loop(0, UB, column, (jnp.int32(-1), jnp.int32(0)))


def pack_core(first, last, meta, child):
    def body(ins, held, sem):
        meta, child = ins[:2]
        core = meta[UB + 1] & 1
        for wait in (False, True):
            def act(j, owner, rank, wait=wait):
                @pl.when((rank >= first) & (rank < last) & ((owner & 1) != core))
                def _():
                    columns = pl.ds(pl.multiple_of(j * BLK, BLK), BLK)
                    one = copy(child.at[:, :, columns], held.at[0, rank - first, owner >> 1], sem)
                    one.wait() if wait else one.start()

            own_columns(meta, act)

    return call(body, [meta, child], [(last - first, 8, 2, BLK, BLK)], "pack_core")


def pack_x(first, last, meta, child, crossed, base, after):
    def body(ins, held, sem):
        meta, child, crossed = ins[:3]
        front = meta[UB + 1]
        x, core = (front >> 1) & 3, front & 1
        for wait in (False, True):
            def act(j, owner, rank, wait=wait):
                @pl.when((rank >= first) & (rank < last) & ((owner & 1) == core))
                def _():
                    source = child.at[:, :, pl.ds(pl.multiple_of(j * BLK, BLK), BLK)]
                    d = copy(source, held.at[((owner >> 1) - x) & 3, rank - first, owner >> 3, 0], sem)
                    d.wait() if wait else d.start()

            def other(f, carry, wait=wait):
                for rank in range(first, last):
                    @pl.when(meta[COUNT + f * 2 + core] > rank)
                    def _():
                        d = copy(crossed.at[rank - base, f], held.at[(f - x) & 3, rank - first, f >> 2, 1], sem)
                        d.wait() if wait else d.start()

                return carry

            own_columns(meta, act)
            lax.fori_loop(0, 8, other, 0)

    return call(body, [meta, child, crossed] + after, [(last - first, 2, 2, 2, BLK, BLK)] * 4, "pack_x")


def pack_y(c, tab, arrays, base, extra=None):
    def body(ins, held, sem):
        tab, arrays = ins[0], ins[1:]
        leaf, front = tab[0], tab[1]
        y_hi, x, core = front >> 3, (front >> 1) & 3, front & 1
        for wait in (False, True):
            for to_hi in range(2):
                @pl.when(tab[T_M + leaf * 16 + to_hi * 8 + (front & 7)] > c)
                def _():
                    for k in range(4):
                        def one(n, carry):
                            other, r = n >> 1, n & 1
                            slot = (((x - k) & 3) * 2 + (core ^ other)) * 2 + r
                            owner = tab[T_R + leaf * UB + y_hi * 16 + slot]
                            d = copy(arrays[k].at[c - base, to_hi, other, r], held.at[0, to_hi * 2 + (owner >> 2), slot], sem)
                            d.wait() if wait else d.start()
                            return carry

                        lax.fori_loop(0, 4, one, 0)

            if extra is not None:
                to = held.at[0, (1 - y_hi) * 2 + (leaf >> 2)]
                for h in range(2):
                    columns = pl.ds(h * BLK, BLK)
                    for source, target in (
                        (arrays[4].at[pl.ds(0, BLK), columns], to.at[16 + h]),
                        (arrays[4].at[pl.ds(BLK, 64), columns], to.at[18, pl.ds(h * 64, 64)]),
                    ):
                        d = copy(source, target, sem)
                        d.wait() if wait else d.start()

    arrays = arrays if extra is None else arrays + [extra]
    return call(body, [tab] + arrays, [(4, 16 if extra is None else 19, BLK, BLK)], "pack_y")[0]


def pack_z(c, tab, array, extra=None):
    def body(ins, held, sem):
        tab, array = ins[:2]
        leaf, front = tab[0], tab[1]
        z, y_lo = leaf & 3, leaf >> 2
        for wait in (False, True):
            for source in range(4):
                from_lo = source & 1
                group = from_lo * 4 + z

                @pl.when(tab[T_M + group * 16 + front] > c)
                def _():
                    def one(s, carry):
                        i = group * UB + (source >> 1) * 16 + s
                        owner = tab[T_R + i]

                        @pl.when((owner >> 2) == y_lo)
                        def _():
                            d = copy(array.at[source, s], held.at[(owner - z) & 3, from_lo, tab[T_RANK + i]], sem)
                            d.wait() if wait else d.start()

                        return carry

                    lax.fori_loop(0, 16, one, 0)

            if extra is not None:
                for k in range(4):
                    for h in range(2):
                        d = copy(ins[2].at[:, pl.ds(h * BLK, BLK)], held.at[k, h, 8], sem)
                        d.wait() if wait else d.start()

    more = [] if extra is None else [extra]
    return call(body, [tab, array] + more, [(2, 8 + len(more), BLK, BLK)] * 4, "pack_z")


def pack_panel(meta, child, front_tile):
    def body(ins, held, sem):
        meta, child, tile = ins
        leaf, front = meta[UB], meta[UB + 1]
        for wait in (False, True):
            def go(source, at):
                d = copy(source, held.at[(0,) + at], sem)
                d.wait() if wait else d.start()

            for j in range(NPAN):
                @pl.when(meta[j] < NPAN)
                def _():
                    for r in range(2):
                        go(child.at[r, :, pl.ds(j * BLK, BLK)], (meta[front * 2 + r] >> 4, r * NPAN + meta[j]))

            @pl.when((front == 0) & (meta[0] == 0) & (meta[1] == 1))
            def _():
                for t in range(8):
                    go(child.at[1, :, pl.ds(0, BLK)], (t, 4))

            @pl.when((front == 0) & (leaf == 0))
            def _():
                for t in range(8):
                    go(tile.at[pl.ds(BLK, BLK), pl.ds(0, BLK)], (t, 5))

    return call(body, [meta, child, front_tile], [(8, 6, BLK, BLK)], "pack_panel")[0]


def panel_part(flat, front_tile, arrived):
    def kernel(flat, tile, arrived, o0, o1, total, held, sem, tile_sem):
        leaf, front = flat[256], flat[257]
        y_hi, x, core = front >> 3, (front >> 1) & 3, front & 1
        come = copy(arrived, held, sem)
        come.start()

        def place(u):
            return (u & 1) ^ core, (((u >> 1) & 3) - x) & 3, pl.ds(pl.multiple_of(((u >> 3) ^ y_hi) * BLK, BLK), BLK)

        def rows(act):
            def one(u, carry):
                act(copy(tile.at[pl.ds(pl.multiple_of(u * BLK, BLK), BLK), pl.ds(0, NPAN * BLK)], total.at[place(u)], tile_sem))
                return carry

            lax.fori_loop(0, 16, one, 0)

        @pl.when(front == 0)
        def _():
            rows(lambda d: d.start())
            rows(lambda d: d.wait())

        @pl.when(front != 0)
        def _():
            total[...] = jnp.zeros_like(total)

        come.wait()

        @pl.when(front == 0)
        def _():
            for k in range(8):
                for h in range(2):
                    total[k // 4, k % 4, pl.ds(256, 64), pl.ds(h * BLK, BLK)] = held[0, 5, pl.ds(h * 64, 64)]

            def corner(g, carry):
                @pl.when((flat[g * UB] == 0) & (flat[g * UB + 1] == 1))
                def _():
                    for k in range(8):
                        for h in range(2):
                            total[k // 4, k % 4, pl.ds(256, 64), pl.ds(h * BLK, BLK)] += held[g, 4, pl.ds(h * 64, 64)]

                return carry

            lax.fori_loop(0, 8, corner, 0)

        def add(n, carry):
            g, r = n >> 1, n & 1
            parent = flat[g * UB + front * 2 + r]

            @pl.when((parent >> 4) == leaf)
            def _():
                other, k, at = place(parent & 15)
                for v in range(NPAN):
                    @pl.when((flat[g * UB] == v) | (flat[g * UB + 1] == v))
                    def _():
                        total[other, k, at, pl.ds(v * BLK, BLK)] += held[g, r * NPAN + v]

            return carry

        lax.fori_loop(0, 16, add, 0)
        out = [copy(total.at[k], o, sem) for k, o in enumerate((o0, o1))]
        for o in out:
            o.start()
        for o in out:
            o.wait()

    block = (4, 2 * BLK + 64, NPAN * BLK)
    return pl.pallas_call(
        kernel,
        out_shape=[jax.ShapeDtypeStruct(block, jnp.float32)] * 2,
        in_specs=[SMEM, HBM, HBM],
        out_specs=[HBM] * 2,
        scratch_shapes=[
            pltpu.VMEM((2,) + block, jnp.float32),
            pltpu.VMEM((8, 6, BLK, BLK), jnp.float32),
            pltpu.SemaphoreType.DMA(()),
            pltpu.SemaphoreType.DMA(()),
        ],
        compiler_params=pltpu.CompilerParams(vmem_limit_bytes=VMEM),
        cost_estimate=COST,
        name="panel_part",
    )(flat, front_tile, arrived)


def product(a, b, precision=lax.Precision.HIGHEST):
    return lax.dot_general(a, b, (((1,), (1,)), ((), ())), precision=precision, preferred_element_type=jnp.float32)


def factors(tab, block_inv, corner, sources, sides, of_rows):
    n = len(sources)
    blocks = 8

    def kernel(tab, inv, corner, *refs):
        sources, outs = refs[:n], refs[n:]
        leaf, front = tab[0], tab[1]
        below = product(corner[...], inv[0])
        for side, source in zip(sides, sources):
            for k in range(4):
                for m in range(2 if of_rows else 1):
                    if of_rows:
                        at = ((front >> 3) ^ side) * 8 + (((front >> 1) - k) & 3) * 2 + ((front & 1) ^ m)
                        raw = source[k, m]
                    else:
                        at = ((leaf >> 2) ^ side) * 4 + ((leaf - k) & 3)
                        raw = source[k]
                    first = ((leaf if of_rows else front) == 0) & (at == 0)
                    one = product(raw[:, :BLK], inv[0])
                    two = product(raw[:, BLK:] - product(one, below), inv[1])
                    two = jnp.where(first, 0.0, two)
                    rows = pl.ds(pl.multiple_of((at & 7) * BLK, BLK), BLK)
                    for h, part in enumerate((one, two)):
                        high = part.astype(jnp.bfloat16)
                        low = (part - high.astype(jnp.float32)).astype(jnp.bfloat16)
                        for t, value in enumerate((high, low, high) if of_rows else (high, high, low)):
                            outs[0][rows, pl.ds((t * 2 + h) * BLK, BLK)] = value
                        if of_rows:
                            outs[1][rows, pl.ds(h * BLK, BLK)] = part

    vmem = pl.BlockSpec(memory_space=pltpu.VMEM)
    shapes = [jax.ShapeDtypeStruct((blocks * BLK, 6 * BLK), jnp.bfloat16)]
    if of_rows:
        shapes.append(jax.ShapeDtypeStruct((blocks * BLK, 2 * BLK), jnp.float32))
    return pl.pallas_call(
        kernel,
        out_shape=shapes,
        in_specs=[SMEM] + [vmem] * (2 + n),
        out_specs=[vmem] * len(shapes),
        compiler_params=pltpu.CompilerParams(vmem_limit_bytes=VMEM),
        cost_estimate=COST,
        name="factors",
    )(tab, block_inv, corner, *sources)


def accumulate(chunks, tab, tile, arrays, panel=None):
    n_arrays = 4 * len(chunks)
    width = tile.shape[1]
    ranks = sorted({c for c, _, _ in chunks})
    steps = tile.shape[0] // (BLK * STEP)
    half = steps // 2

    def kernel(tab, tile, *refs):
        arrays, refs = refs[:n_arrays], refs[n_arrays:]
        if panel is not None:
            (near, near_plain, far, far_plain, right), refs = refs[:5], refs[5:]
        out, held, sems = refs
        i = pl.program_id(0)
        z = tab[0] & 3

        def each(step, act):
            for r in range(STEP):
                for g in range(8):
                    group = g // 4 * 4 + ((z - g) & 3)
                    p = tab[T_PROW + group * 16 + step * STEP + r]

                    @pl.when(p >= 0)
                    def _():
                        for m, c in enumerate(ranks):
                            v = tab[T_VCOL + group * 4 + c]

                            @pl.when(v >= 0)
                            def _():
                                act(r, g, p, m, c, v)

        def fetch(step, wait):
            slot = step & 1

            def act(r, g, p, m, c, v):
                for n, (cc, off, rows) in enumerate(chunks):
                    if cc == c:
                        source = arrays[n * 4 + g % 4].at[g // 4, p]
                        one = copy(source, held.at[slot, r, g, m, pl.ds(off, rows)], sems.at[slot])
                        one.wait() if wait else one.start()

            each(step, act)

        @pl.when(i == 0)
        def _():
            fetch(0, False)

        @pl.when(i + 1 < steps)
        def _():
            fetch(i + 1, False)

        if panel is None:
            out[...] = tile[...]
        else:
            mine = (i // half) == (tab[1] >> 3)
            out[...] = tile[...] - product(jnp.where(mine, near[...], far[...]), right[...], None)
        fetch(i, True)
        slot = i & 1

        def add(r, g, p, m, c, v):
            out[pl.ds(r * BLK, BLK), pl.ds(pl.multiple_of(v * BLK, BLK), BLK)] += held[slot, r, g, m]

        each(i, add)
        if panel is not None:
            @pl.when(tab[1] == 0)
            def _():
                out[:, pl.ds(0, 2 * BLK)] = jnp.where(mine, near_plain[...], far_plain[...])

    rows = BLK * STEP
    specs = [SMEM, pl.BlockSpec((rows, width), lambda i: (i, 0))] + [HBM] * n_arrays
    operands = [tab, tile] + list(arrays)
    if panel is not None:
        specs += [
            pl.BlockSpec((rows, 6 * BLK), lambda i: (i % half, 0)),
            pl.BlockSpec((rows, 2 * BLK), lambda i: (i % half, 0)),
        ] * 2 + [pl.BlockSpec((width, 6 * BLK), lambda i: (0, 0))]
        operands += list(panel)
    return pl.pallas_call(
        kernel,
        out_shape=jax.ShapeDtypeStruct(tile.shape, jnp.float32),
        grid=(steps,),
        in_specs=specs,
        out_specs=pl.BlockSpec((rows, width), lambda i: (i, 0)),
        scratch_shapes=[
            pltpu.VMEM((2, STEP, 8, len(ranks), BLK, BLK), jnp.float32),
            pltpu.SemaphoreType.DMA((2,)),
        ],
        compiler_params=pltpu.CompilerParams(vmem_limit_bytes=VMEM),
        cost_estimate=COST,
        name="accumulate" if panel is None else "final",
    )(*operands)


def shift_x(a, dx, dc):
    pairs = [
        (front_at(h, x, c), front_at(h, x + dx, c + dc)) for h in range(2) for x in range(4) for c in range(2)
    ]
    return lax.ppermute(a, "front", pairs)


def exchange_y(a):
    groups = [
        [device_at(leaf_at(y, z), front_at(y // 2, x, c)) for y in range(4)]
        for z in range(4) for x in range(4) for c in range(2)
    ]
    return lax.all_to_all(a, ("leaf", "front"), 0, 0, axis_index_groups=groups, tiled=True)


def shift_z(a, dz):
    return lax.ppermute(a, "leaf", [(leaf_at(l, z), leaf_at(l, z + dz)) for l in range(2) for z in range(4)])


def tie(values, *after):
    return list(lax.optimization_barrier(tuple(values) + after)[:len(values)])


def other_device(a, bit):
    return lax.ppermute(a, ("leaf", "front"), [(d, d ^ bit) for d in range(128)])


OTHER_CORE, OTHER_Y_HI, OTHER_Y_LO = 1, 8, 64


def tables(assembly, leaf, front):
    col_owner, row_owner = assembly >> 3, assembly >> 4
    earlier = jnp.arange(UB)[:, None] > jnp.arange(UB)[None, :]

    def rank(owner):
        same = (owner[:, :, None] == owner[:, None, :]) & earlier[None]
        return jnp.sum(same.astype(jnp.int32), axis=2)

    def pick(match, value):
        return jnp.sum(jnp.where(match, value + 1, 0), axis=1).astype(jnp.int32) - 1

    row_rank, col_rank = rank(row_owner), rank(col_owner)
    count = jnp.sum((col_owner[:, :, None] == jnp.arange(16)).astype(jnp.int32), axis=1)
    mine = row_owner == leaf
    row_u = pick(
        mine[:, :, None] & (row_rank[:, :, None] == jnp.arange(8)), (assembly & 15)[:, :, None]
    )
    row_p = pick(assembly[:, :, None] == leaf * 16 + jnp.arange(16), row_rank[:, :, None])
    col_v = pick(
        (col_owner == front)[:, :, None] & (col_rank[:, :, None] == jnp.arange(CAPF)), (assembly & 7)[:, :, None]
    )
    head = jnp.concatenate([leaf[None], front[None], jnp.zeros((T_R - 2,), jnp.int32)])
    parts = [head] + [t.reshape(-1) for t in (row_owner, row_rank, count, row_u, row_p, col_v)]
    size = sum(t.shape[0] for t in parts)
    return jnp.concatenate(parts + [jnp.zeros((T_ALL - size,), jnp.int32)])


def per_device(child_update, assembly, front_matrix, block_inv):
    leaf, front = lax.axis_index("leaf"), lax.axis_index("front")
    child = child_update.reshape(2, BLK, child_update.shape[2])
    own = lax.dynamic_index_in_dim(assembly, leaf, 0, keepdims=False)
    count = jnp.sum(((own >> 3)[:, None] == jnp.arange(16)).astype(jnp.int32), axis=0)
    meta = jnp.concatenate([own, leaf[None], front[None], jnp.zeros((COUNT - UB - 2,), jnp.int32), count])
    tab = tables(assembly, leaf, front)

    flat = jnp.concatenate([assembly.reshape(-1), leaf[None], front[None], jnp.zeros((126,), jnp.int32)])
    n = CAPF

    arrived = lax.all_to_all(pack_panel(meta, child, front_matrix), "leaf", 0, 0, tiled=True)
    first = shift_x(pack_core(0, 1, meta, child)[0], 0, 1)
    rest = shift_x(pack_core(1, n, meta, child)[0], 0, 1)

    outs = pack_x(0, 1, meta, child, first, 0, [])
    x_in = [[outs[0]] + [shift_x(outs[k], k, 0) for k in range(1, 4)]]
    outs = pack_x(1, 2, meta, child, rest, 1, x_in[0][1:])
    x_in.append([outs[0]] + [shift_x(outs[k], k, 0) for k in range(1, 4)])
    mine, others = panel_part(tie([flat], outs[0])[0], front_matrix, arrived)
    mine = mine + other_device(others, OTHER_CORE)
    parts = [mine[k] for k in range(4)]
    parts = [parts[0]] + [shift_x(a, k + 1, 0) for k, a in enumerate(tie(parts[1:], x_in[1][1], x_in[1][3]))]
    *parts, x_in[1][2] = tie(parts + [x_in[1][2]])
    outs = pack_x(2, n, meta, child, rest, 1, x_in[1][1:] + parts[1:])
    x_in.append([outs[0]] + [shift_x(outs[k], k, 0) for k in range(1, 4)])
    part = parts[0] + parts[1] + parts[2] + parts[3]
    kept = jnp.concatenate([part[:BLK], part[256:]])
    sent = part[BLK:]
    bases = (0, 1, 2, 2)
    y_in, z_out, z_in, gates = [], [], [], [[arrived], [], [], [], []]

    for s in range(n):
        if s == 1:
            sent = tie([sent], z_out[0][0])[0]
        packed = pack_y(s, tab, x_in[min(s, 2)], bases[s], sent if s == 1 else None)
        before = ([y_in[s - 1]] if s else []) + (z_in[s - 2][1:] if s > 1 else []) + gates[s]
        y_in.append(exchange_y(tie([packed], *before)[0]))
        if s == 1:
            got = lax.dynamic_index_in_dim(y_in[1][:, 16:], (1 - (front >> 3)) * 2 + (leaf >> 2), 0, keepdims=False)
            corner = jnp.concatenate([kept[BLK:, :BLK], kept[BLK:, BLK:]]) + got[2]
            part = kept[:BLK] + jnp.concatenate([got[0], got[1]], axis=1)
            near = jnp.stack([part, other_device(part, OTHER_CORE)])
            near = jnp.stack([near] + [shift_x(near, k, 0) for k in range(1, 4)])
            pairs = [(b, device_at(b % 8, b // 8)) for b in range(128)]
            moved = lax.ppermute(part, ("leaf", "front"), pairs)
            gates[3] += [near, moved]
        before = z_in[s - 1][1:] if s else []
        z_out.append(pack_z(s, tab, tie([y_in[s]], *before)[0] if before else y_in[s], moved if s == 2 else None))
        z_in.append([z_out[s][0]] + [shift_z(z_out[s][k], k) for k in range(1, 4)])

    columns_near = jnp.stack([jnp.concatenate([z_in[2][k][0, 8], z_in[2][k][1, 8]], axis=1) for k in range(4)])
    near_late, columns_late = tie([near, columns_near], z_out[n - 1][0])
    far = other_device(near_late, OTHER_Y_HI)
    columns_far = other_device(columns_late, OTHER_Y_LO)
    left = factors(tab, block_inv, corner, [near], [0], True)
    tile = accumulate(WHOLE[:3], tab, front_matrix, z_in[0] + z_in[1] + z_in[2])
    left = left + factors(tab, block_inv, corner, [far], [1], True)
    columns_far = tie([columns_far], left[2], tile)[0]
    right = factors(tab, block_inv, corner, [columns_near, columns_far], [0, 1], False)
    return accumulate(WHOLE[3:], tab, tile, z_in[3], left + right)


def solution(mesh):
    placed = (P("leaf", "front", None), P(), P("leaf", "front"), P())
    return jax.shard_map(
        per_device, mesh=mesh, in_specs=placed, out_specs=P("leaf", "front"), check_vma=False
    )
```
